128 devices in a mesh: task: 8 (over y, z_hi), width: 16 (over z_lo, x, core).
Axes of the slice: x: 4, y: 4, z: 4 (z_hi: 2, z_lo: 2; z = z_hi * 2 + z_lo), core: 2. Of those that a mesh axis runs over, the one named last changes fastest.
Arguments:
- task_ids: int32 [1024], P('task'), may hold values from 0 to 1023
- embed_table: bfloat16 [1024, 1024], replicated, may hold values from -6 to 6
- trunk_weight: bfloat16 [1024, 2048], replicated, may hold values from -0.1875 to 0.1875
- trunk_bias: float32 [2048], replicated, may hold values from -6 to 6
- head_weight: bfloat16 [2048, 262144], P(None, ('task', 'width')), may hold values from -0.125 to 0.125
- head_bias: float32 [262144], P(('task', 'width')), may hold values from -4 to 4
- token_row: int32 [32768], P('task'), may hold values from 0 to 1023, as said below
- inputs: bfloat16 [32768, 8192], P('task', 'width'), may hold values from -6 to 6
- frozen: bfloat16 [32768, 8192], P('task', 'width'), may hold values from -6 to 6
Outputs:
- adapted: bfloat16 [32768, 8192], P('task', 'width')
The draws below stay inside these ranges and needn't reach their ends.
Inputs may be any that keep to these rules, and one draw needn't show every extreme that they name: `token_row`: each of the 1024 rows is named by exactly 32 tokens, and tokens b * 4096 to (b + 1) * 4096 - 1 name only rows b * 128 to (b + 1) * 128 - 1.
All inputs are finite; a program needn't handle non-finite values.
Results may differ from the reference program's by a relative error of at most 0.0061.
Values may be sent and summed in bfloat16 or wider, within the bound.
No kernel may reach another device: no remote copies, remote signals or barrier semaphores. Data moves between devices by JAX's collectives and lax.ppermute only.
A program may use at most 128 MiB of HBM per device.

```python
import math
import jax
import jax.numpy as jnp
from jax import lax

TABLE = 1024
EMB = 1024
HID = 2048
WIDTH = 8192
RANK = 16
TOK_ROW = 32
ROWS_DEV = 128
ROWS = 1024
TOK_DEV = 4096
TOKENS = 32768
COLS = 262144
N_WIDTH = 16


def draw_token_row(key, part):
    block_count = ROWS // ROWS_DEV
    key_list = jax.random.split(key, block_count)
    shuffled = jax.vmap(lambda subkey: jax.random.permutation(subkey, TOK_DEV))(key_list)
    local_rows = (shuffled % ROWS_DEV).astype(jnp.int32)
    offsets = jnp.arange(block_count, dtype=jnp.int32)[:, None] * ROWS_DEV
    return (local_rows + offsets).reshape(-1).astype(jnp.int32)


def with_ends(entries, own_key, least, top_value):
    spot = [jax.random.randint(jax.random.fold_in(own_key, axis), (), 0, length) for axis, length in enumerate(entries.shape)]
    widest = entries.shape.index(max(entries.shape))
    next_to = spot[:widest] + [(spot[widest] + 1) % entries.shape[widest]] + spot[widest + 1:]
    return entries.at[tuple(spot)].set(least).at[tuple(next_to)].set(top_value)


def block_levels(stream_key, shape, cuts, least, high):
    def one(axis_at, shards_of):
        steps = jax.random.uniform(jax.random.fold_in(jax.random.fold_in(stream_key, 6), axis_at), (shards_of,), jnp.float32, least / len(cuts), high / len(cuts))
        return jnp.repeat(jnp.exp(steps), shape[axis_at] // shards_of).reshape((-1,) + (1,) * (len(shape) - axis_at - 1))

    gain = one(*cuts[0])
    for cut in cuts[1:]:
        gain = gain * one(*cut)
    return gain


def bell_draw(own_key, extent, width, most, pieces=(), kind=jnp.bfloat16):
    gain = block_levels(own_key, extent, pieces, -0.22, 0.18) if pieces else 1.0
    array = jax.random.normal(own_key, extent, jnp.float32) * width * gain
    return jnp.minimum(jnp.maximum(array, -most), most).astype(kind)


def setup_inputs(seed: int = 0) -> dict:
    streams_of = jax.random.split(jax.random.key(seed), 10)
    return {
        "task_ids": with_ends(jax.random.randint(streams_of[0], (ROWS,), 0, TABLE), jax.random.fold_in(streams_of[0], 1), 0, TABLE - 1).astype(jnp.int32),
        "embed_table": bell_draw(streams_of[1], (TABLE, EMB), 1.0, 6.0),
        "trunk_weight": bell_draw(streams_of[2], (EMB, HID), EMB ** -0.5, 0.1875),
        "trunk_bias": bell_draw(streams_of[3], (HID,), 1.0, 6.0, (), jnp.float32),
        "head_weight": bell_draw(streams_of[4], (HID, COLS), HID ** -0.5, 0.125, ((1, 128),)),
        "head_bias": bell_draw(streams_of[5], (COLS,), 0.5, 4.0, ((0, 128),), jnp.float32),
        "token_row": draw_token_row(jax.random.fold_in(streams_of[9], 71), 0),
        "inputs": bell_draw(streams_of[7], (TOKENS, WIDTH), 1.0, 6.0, ((0, 8), (1, 16))),
        "frozen": bell_draw(streams_of[8], (TOKENS, WIDTH), 1.0, 6.0, ((0, 8), (1, 16))),
    }


def reference(task_ids, embed_table, trunk_weight, trunk_bias, head_weight, head_bias, token_row, inputs, frozen):
    one_hot = (task_ids[:, None] == jnp.arange(TABLE, dtype=jnp.int32)[None, :]).astype(jnp.bfloat16)
    embedded = jnp.dot(one_hot, embed_table, preferred_element_type=jnp.float32).astype(jnp.bfloat16)
    preact = jnp.dot(embedded, trunk_weight, preferred_element_type=jnp.float32) + trunk_bias
    hidden = jax.nn.silu(preact).astype(jnp.bfloat16)
    factors = (jnp.dot(hidden, head_weight, preferred_element_type=jnp.float32) + head_bias).astype(jnp.bfloat16)
    slice_width = WIDTH // N_WIDTH
    grouped = factors.reshape(ROWS, 2, RANK, slice_width, N_WIDTH).transpose(0, 1, 2, 4, 3).reshape(ROWS, 2, RANK, WIDTH)
    entry_all = grouped[:, 0]
    exit_all = grouped[:, 1]
    inv_width = 1.0 / math.sqrt(WIDTH)
    inv_rank = 1.0 / math.sqrt(RANK)
    block_size = TOK_ROW * math.gcd(ROWS_DEV, 8)
    block_total = TOKENS // block_size

    def adapt_block(block_data):
        tokens_in, frozen_in, rows_in = block_data
        entry_tok = entry_all[rows_in].astype(jnp.float32)
        exit_tok = exit_all[rows_in].astype(jnp.float32)
        coef = jnp.einsum('te,tre->tr', tokens_in.astype(jnp.float32), entry_tok, precision=lax.Precision.HIGHEST)
        coef = (coef * inv_width).astype(jnp.bfloat16)
        update = jnp.einsum('tr,tre->te', coef.astype(jnp.float32), exit_tok, precision=lax.Precision.HIGHEST)
        return (frozen_in.astype(jnp.float32) + update * inv_rank).astype(jnp.bfloat16)
    result = lax.map(adapt_block, (inputs.reshape(block_total, block_size, WIDTH), frozen.reshape(block_total, block_size, WIDTH), token_row.reshape(block_total, block_size)))
    return result.reshape(TOKENS, WIDTH)
```

```python
import math

import jax
import jax.numpy as jnp
from jax import lax
from jax.experimental import pallas as pl
from jax.experimental.pallas import tpu as pltpu
from jax.sharding import PartitionSpec as P

WIDTH = 8192
RANK = 16
LANES = 128
BOTH = ("task", "width")
BF16 = jnp.bfloat16
F32 = jnp.float32


def product(a, b, a_dim=1, b_dim=0):
    return lax.dot_general(a, b, (((a_dim,), (b_dim,)), ((), ())), preferred_element_type=F32)


def iota(shape, dim):
    return lax.broadcasted_iota(jnp.int32, shape, dim)


def one_where(test):
    return jnp.where(test, 1.0, 0.0).astype(BF16)


def lane_group(rows):
    return (iota((rows, LANES), 1) >> 4).astype(F32).astype(BF16)


def cost(flops, moved):
    return pl.CostEstimate(flops=int(flops), transcendentals=0, bytes_accessed=int(moved))


def head_kernel(low_ref, high_ref, weight_ref, bias_ref, out_ref):
    step = pl.program_id(0)
    half = low_ref.shape[1]
    out = product(low_ref[...], weight_ref[:half, :])
    out = out + product(high_ref[...], weight_ref[half:, :]) + bias_ref[...]
    col = iota((256, 256), 0)
    target = ((col >> 3) & 1) * 128 + ((step + col) & 7) * 16 + (col >> 4)
    perm = one_where(iota((256, 256), 1) == target)
    grouped = product(out.astype(BF16), perm).astype(BF16)
    group = iota((1, LANES), 1) >> 4
    for turn in range(8):
        here = jnp.broadcast_to(one_where(group == ((step + turn) & 7)), (16, LANES)) > 0.5
        for side in range(2):
            dest = side * 8 + turn
            for at in range(0, out.shape[0], 16):
                new = grouped[at : at + 16, side * LANES : side * LANES + LANES]
                out_ref[dest, at : at + 16] = jnp.where(here, new, out_ref[dest, at : at + 16])


def table_factors(low, high, head_weight, bias):
    entries, half = low.shape
    hid, cols = head_weight.shape
    return pl.pallas_call(
        head_kernel,
        grid=(cols // 256,),
        in_specs=[
            pl.BlockSpec((entries, half), lambda i: (0, 0)),
            pl.BlockSpec((entries, half), lambda i: (0, 0)),
            pl.BlockSpec((hid, 256), lambda i: (0, i)),
            pl.BlockSpec((1, 256), lambda i: (0, i)),
        ],
        out_specs=pl.BlockSpec((16, entries, LANES), lambda i: (0, 0, 0)),
        out_shape=jax.ShapeDtypeStruct((16, entries, LANES), BF16),
        cost_estimate=cost(2 * entries * cols * (hid + 256), 2 * hid * cols),
        name="head",
    )(low, high, head_weight, bias)


def pick_kernel(me_ref, id_ref, table_ref, out_ref, hot_ref):
    step = pl.program_id(0)
    tasks, rows, _ = id_ref.shape
    entries = table_ref.shape[1]

    @pl.when(step == 0)
    def _():
        lane = iota((rows, LANES), 1)
        for task in range(tasks):
            ids = id_ref[task ^ me_ref[0]]
            for at in range(0, entries, LANES):
                hot_ref[task * rows : (task + 1) * rows, at : at + LANES] = one_where(
                    ids == lane + at
                )

    pair = jnp.concatenate([table_ref[0], table_ref[1]], axis=1)
    picked = product(hot_ref[...], pair)
    for side in range(2):
        turn = (2 * step + side) & 7
        piece = pltpu.roll(picked[:, side * LANES : side * LANES + LANES], (8 - turn) * 16, 1)
        out_ref[:, side] = piece.astype(BF16).reshape(tasks, rows, LANES)


def picked_rows(me, ids, factors):
    tasks, rows = ids.shape
    dests, entries, _ = factors.shape
    id_grid = jnp.broadcast_to(ids[:, :, None], (tasks, rows, LANES))
    return pl.pallas_call(
        pick_kernel,
        grid=(dests // 2,),
        in_specs=[
            pl.BlockSpec(memory_space=pltpu.SMEM),
            pl.BlockSpec((tasks, rows, LANES), lambda i: (0, 0, 0)),
            pl.BlockSpec((2, entries, LANES), lambda i: (i, 0, 0)),
        ],
        out_specs=pl.BlockSpec((tasks, 2, rows, LANES), lambda i: (0, i, 0, 0)),
        out_shape=jax.ShapeDtypeStruct((tasks, dests, rows, LANES), BF16),
        scratch_shapes=[pltpu.VMEM((tasks * rows, entries), BF16)],
        cost_estimate=cost(2 * tasks * rows * entries * dests * LANES, 8 << 20),
        name="pick",
    )(me, id_grid, factors)


def sort_kernel(all_ref, row_ref, in_ref, out_ref, low_ref, part_ref, name_ref, rank_ref, slot_ref):
    step = pl.program_id(0)
    tokens = all_ref.shape[1]
    tile = out_ref.shape[0]
    count = 128
    per_row = tokens // count

    @pl.when(step == 0)
    def _():
        before = one_where(iota((256, 256), 0) < iota((256, 256), 1))
        carry = jnp.zeros((count, 1), F32)
        for at in range(0, tokens, 256):
            rows = all_ref[:, at : at + 256]
            hot = jnp.where(iota((count, 256), 0) == rows, 1.0, 0.0)
            seen = product(hot.astype(BF16), before) + carry
            rank = jnp.sum(hot * seen, axis=0, keepdims=True).astype(jnp.int32)
            carry = carry + jnp.sum(hot, axis=1, keepdims=True)
            slot = rows * per_row + rank
            slot_ref[:, at : at + 256] = slot
            rank_ref[at // 256] = slot

    total = jnp.zeros(out_ref.shape, F32)
    for at in range(0, tokens, 1024):
        place = iota((tile, 1024), 0) + step * tile
        hot = one_where(place == slot_ref[:, at : at + 1024])
        total = total + product(hot, in_ref[at : at + 1024, :])
    out_ref[...] = total.astype(BF16)

    for at in range(0, tile, 256):
        slot = rank_ref[step * (tile // 256) + at // 256]
        slot = jnp.broadcast_to(slot.astype(F32), (LANES, 256)).T.astype(jnp.int32)
        span = slice(at, at + 256)
        lane = iota((256, LANES), 1)
        low_ref[span, :LANES] = one_where((slot & 255) == lane)
        low_ref[span, LANES:] = one_where((slot & 255) == lane + LANES)
        part_ref[span, :] = (slot >> 8).astype(F32).astype(BF16)
        name_ref[span, :] = (slot // per_row).astype(F32).astype(BF16)


def sorted_tokens(local_row, inputs):
    tokens, width = inputs.shape
    tile = 512
    wide = lambda lanes: jax.ShapeDtypeStruct((tokens, lanes), BF16)
    return pl.pallas_call(
        sort_kernel,
        grid=(tokens // tile,),
        in_specs=[
            pl.BlockSpec((1, tokens), lambda i: (0, 0)),
            pl.BlockSpec((1, tile), lambda i: (0, i)),
            pl.BlockSpec((tokens, width), lambda i: (0, 0)),
        ],
        out_specs=[
            pl.BlockSpec((tile, width), lambda i: (i, 0)),
            pl.BlockSpec((tile, 256), lambda i: (i, 0)),
            pl.BlockSpec((tile, LANES), lambda i: (i, 0)),
            pl.BlockSpec((tile, LANES), lambda i: (i, 0)),
        ],
        out_shape=[wide(width), wide(256), wide(LANES), wide(LANES)],
        scratch_shapes=[
            pltpu.VMEM((tokens // 256, 1, 256), jnp.int32),
            pltpu.VMEM((1, tokens), jnp.int32),
        ],
        cost_estimate=cost(2 * tokens * tokens * width, 16 << 20),
        name="sort",
    )(local_row, local_row, inputs)


def entry_kernel(in_ref, block_ref, out_ref):
    slots = in_ref.shape[0]
    part = block_ref.shape[3]
    factor = jnp.concatenate(
        [block_ref[0, :, q].reshape(RANK * part, LANES) for q in range(4)], axis=1
    )
    scores = product(factor, in_ref[...], 1, 1).reshape(RANK, part, slots)
    match = iota((part, slots), 0) == iota((part, slots), 1) // (slots // part)
    coef = jnp.sum(jnp.where(match[None], scores, 0.0), axis=1)
    for at in range(out_ref.shape[0]):
        out_ref[at] = coef[:, at * 256 : (at + 1) * 256]


def rank_parts(inputs, blocks):
    tokens, width = inputs.shape
    rows = blocks.shape[3]
    part = 16
    steps = rows // part
    tile = tokens // steps
    return pl.pallas_call(
        entry_kernel,
        grid=(steps,),
        in_specs=[
            pl.BlockSpec((tile, width), lambda i: (i, 0)),
            pl.BlockSpec((1, RANK, 4, part, LANES), lambda i: (0, 0, 0, i, 0)),
        ],
        out_specs=pl.BlockSpec((tile // 256, RANK, 256), lambda i: (i, 0, 0)),
        out_shape=jax.ShapeDtypeStruct((tokens // 256, RANK, 256), F32),
        name="entry",
    )(inputs, blocks)


def order_kernel(block_ref, out_ref):
    out_at = iota((256, 256), 0)
    perm = one_where(iota((256, 256), 1) == (out_at & 15) * 16 + (out_at >> 4))
    piece = jnp.concatenate(
        [block_ref[0, :, q].reshape(RANK * 16, LANES) for q in range(4)], axis=1
    )
    out_ref[...] = product(perm, piece).astype(BF16)


def ordered_exit(blocks):
    rows = blocks.shape[3]
    return pl.pallas_call(
        order_kernel,
        grid=(rows // 16,),
        in_specs=[pl.BlockSpec((1, RANK, 4, 16, LANES), lambda i: (1, 0, 0, i, 0))],
        out_specs=pl.BlockSpec((256, 4 * LANES), lambda i: (i, 0)),
        out_shape=jax.ShapeDtypeStruct((rows * RANK, 4 * LANES), BF16),
        name="order",
    )(blocks)


def exit_kernel(coef_ref, low_ref, part_ref, name_ref, base_ref, factor_ref, out_ref):
    tile = base_ref.shape[0]
    depth = factor_ref.shape[0]
    group = lane_group(tile)
    zero = jnp.zeros((tile, LANES), F32)
    values = product(low_ref[...], coef_ref[...], 1, 1)
    part = part_ref[...].astype(F32)
    group32 = group.astype(F32)
    mine = jnp.where(part == group32, values[:, :LANES], zero)
    mine = mine + jnp.where(part == group32 + 8.0, values[:, LANES:], zero)
    fold = one_where((iota((LANES, LANES), 0) & 15) == (iota((LANES, LANES), 1) & 15))
    coef = product(mine.astype(BF16), fold).astype(BF16)
    name = name_ref[...]
    spread = jnp.concatenate(
        [
            jnp.where(name == group + jnp.asarray(at, BF16), coef, jnp.zeros_like(coef))
            for at in range(0, depth // RANK, 8)
        ],
        axis=1,
    )
    update = product(spread, factor_ref[...])
    base = base_ref[...].astype(F32)
    out_ref[...] = (base + update * (1.0 / math.sqrt(RANK))).astype(BF16)


def apply_update(coefs, low, part, name, base, factors):
    tokens, width = base.shape
    tile = 512
    return pl.pallas_call(
        exit_kernel,
        grid=(tokens // tile,),
        in_specs=[
            pl.BlockSpec(coefs.shape, lambda i: (0, 0)),
            pl.BlockSpec((tile, 256), lambda i: (i, 0)),
            pl.BlockSpec((tile, LANES), lambda i: (i, 0)),
            pl.BlockSpec((tile, LANES), lambda i: (i, 0)),
            pl.BlockSpec((tile, width), lambda i: (i, 0)),
            pl.BlockSpec(factors.shape, lambda i: (0, 0)),
        ],
        out_specs=pl.BlockSpec((tile, width), lambda i: (i, 0)),
        out_shape=jax.ShapeDtypeStruct((tokens, width), BF16),
        name="exit",
    )(coefs, low, part, name, base, factors)


def to_all(shard, axis):
    length = lax.axis_size(axis)
    return lax.all_to_all(
        jnp.broadcast_to(shard[None], (length, *shard.shape)), axis, 0, 0, tiled=True
    )


def gathered(shard, axis):
    length = lax.axis_size(axis)
    held = shard[None]
    step = 1
    while step < length:
        moved = lax.ppermute(held, axis, [(at, at ^ step) for at in range(length)])
        held = jnp.concatenate([held, moved])
        step *= 2
    return held


def on_device(
    task_ids,
    embed_table,
    trunk_weight,
    trunk_bias,
    head_weight,
    head_bias,
    token_row,
    inputs,
    frozen,
):
    tasks = lax.axis_size("task")
    width = lax.axis_size("width")
    rows_dev = task_ids.shape[0]
    me = lax.axis_index("task")
    ids = gathered(task_ids, "task")

    half = trunk_weight.shape[1] // 2
    tables = []
    for cut in (slice(0, half), slice(half, 2 * half)):
        preact = jnp.dot(embed_table, trunk_weight[:, cut], preferred_element_type=F32)
        tables.append(jax.nn.silu(preact + trunk_bias[cut]).astype(BF16))
    factors = table_factors(*tables, head_weight, head_bias.reshape(1, -1))
    blocks = picked_rows(me.reshape(1), ids, factors)
    moved = lax.all_to_all(
        blocks.reshape(tasks * width, rows_dev, LANES), BOTH, 0, 0, tiled=True
    ).reshape(2, RANK, 4, rows_dev, LANES)

    local_row = (token_row - me * rows_dev).reshape(1, -1)
    in_order, low, part, name = sorted_tokens(local_row, inputs)
    parts = rank_parts(in_order, moved)
    pieces = lax.all_to_all(parts, "width", 0, 0, tiled=True)
    coef = (pieces.sum(axis=0) * (1.0 / math.sqrt(WIDTH))).astype(BF16)
    coefs = to_all(coef, "width").reshape(width * RANK, -1)
    return apply_update(coefs, low, part, name, frozen, ordered_exit(moved))


def solution(mesh):
    return jax.shard_map(
        on_device,
        mesh=mesh,
        in_specs=(
            P("task"),
            P(),
            P(),
            P(),
            P(None, BOTH),
            P(BOTH),
            P("task"),
            P("task", "width"),
            P("task", "width"),
        ),
        out_specs=P("task", "width"),
        check_vma=False,
    )
```

```python
import math

import jax
import jax.numpy as jnp
from jax import lax
from jax.experimental import pallas as pl
from jax.experimental.pallas import tpu as pltpu
from jax.sharding import PartitionSpec as P

WIDTH = 8192
RANK = 16
LANES = 128
BOTH = ("task", "width")
BF16 = jnp.bfloat16
F32 = jnp.float32


def product(a, b, a_dim=1, b_dim=0):
    return lax.dot_general(a, b, (((a_dim,), (b_dim,)), ((), ())), preferred_element_type=F32)


def iota(shape, dim):
    return lax.broadcasted_iota(jnp.int32, shape, dim)


def one_where(test):
    return jnp.where(test, 1.0, 0.0).astype(BF16)


def lane_group(rows):
    return (iota((rows, LANES), 1) >> 4).astype(F32).astype(BF16)


def cost(flops, moved):
    return pl.CostEstimate(flops=int(flops), transcendentals=0, bytes_accessed=int(moved))


def table_kernel(
    embed_ref, trunk_ref, trunk_bias_ref, weight_ref, bias_ref, out_ref, hidden_ref, group_ref
):
    step = pl.program_id(0)
    entries = embed_ref.shape[0]
    hid = hidden_ref.shape[1]
    wide = trunk_ref.shape[1]
    early = hid // wide
    blocks = group_ref.shape[0]

    @pl.when(step < early)
    def _():
        value = product(embed_ref[...], trunk_ref[...]) + trunk_bias_ref[...]
        at = pl.multiple_of(step * wide, wide)
        hidden_ref[:, pl.ds(at, wide)] = jax.nn.silu(value).astype(BF16)

    @pl.when(step >= early)
    def _():
        block = step - early
        out = product(hidden_ref[...], weight_ref[...]) + bias_ref[...]
        col = iota((256, 256), 0)
        target = ((col >> 3) & 1) * 128 + ((block + col) & 7) * 16 + (col >> 4)
        perm = one_where(iota((256, 256), 1) == target)
        group_ref[block] = product(out.astype(BF16), perm).astype(BF16)

    @pl.when(step == early + blocks - 1)
    def _():
        group = lane_group(16)
        masks = [group == jnp.asarray(place, BF16) for place in range(8)]

        def mix(index, carry):
            span = pl.ds(pl.multiple_of(index * 16, 16), 16)
            for side in range(2):
                lanes = slice(side * LANES, side * LANES + LANES)
                tiles = [group_ref[block, span, lanes] for block in range(8)]
                for turn in range(8):
                    mixed = tiles[0]
                    for block in range(1, 8):
                        mixed = jnp.where(masks[(block + turn) % 8], tiles[block], mixed)
                    out_ref[side * 8 + turn, span] = mixed
            return carry

        lax.fori_loop(0, entries // 16, mix, 0, unroll=4)


def table_factors(embed, trunk, trunk_bias, head_weight, bias):
    entries, width = embed.shape
    hid, cols = head_weight.shape
    early, blocks = hid // 512, cols // 256
    first = lambda i: (0, jnp.minimum(i, early - 1))
    then = lambda i: (0, jnp.maximum(i - early, 0))
    return pl.pallas_call(
        table_kernel,
        grid=(early + blocks,),
        in_specs=[
            pl.BlockSpec(embed.shape, lambda i: (0, 0)),
            pl.BlockSpec((width, 512), first),
            pl.BlockSpec((1, 512), first),
            pl.BlockSpec((hid, 256), then),
            pl.BlockSpec((1, 256), then),
        ],
        out_specs=pl.BlockSpec((16, entries, LANES), lambda i: (0, 0, 0)),
        out_shape=jax.ShapeDtypeStruct((16, entries, LANES), BF16),
        scratch_shapes=[
            pltpu.VMEM((entries, hid), BF16),
            pltpu.VMEM((blocks, entries, 256), BF16),
        ],
        cost_estimate=cost(2 * entries * hid * (width + cols), 18 << 20),
        name="table",
    )(embed, trunk, trunk_bias, head_weight, bias)


def pick_kernel(id_ref, table_ref, out_ref, hot_ref):
    step = pl.program_id(0)
    tasks, rows = id_ref.shape
    dests, entries, _ = table_ref.shape

    @pl.when(step == 0)
    def _():
        lane = iota((rows, LANES), 1).astype(F32)
        for task in range(tasks):
            ids = jnp.broadcast_to(id_ref[task : task + 1, :].astype(F32), (LANES, rows)).T
            for at in range(0, entries, LANES):
                hot_ref[task * rows : (task + 1) * rows, at : at + LANES] = one_where(
                    ids == lane + float(at)
                )

    for at in range(0, dests, 2):
        pair = jnp.concatenate([table_ref[at], table_ref[at + 1]], axis=1)
        picked = product(hot_ref[...], pair)
        for side in range(2):
            turn = (dests * step + at + side) & 7
            piece = picked[:, side * LANES : side * LANES + LANES]
            piece = pltpu.roll(piece, (8 - turn) * 16, 1).astype(BF16)
            out_ref[:, at + side] = piece.reshape(tasks, rows, LANES)


def picked_rows(ids, factors):
    tasks, rows = ids.shape
    dests, entries, _ = factors.shape
    span = 4
    return pl.pallas_call(
        pick_kernel,
        grid=(dests // span,),
        in_specs=[
            pl.BlockSpec(ids.shape, lambda i: (0, 0)),
            pl.BlockSpec((span, entries, LANES), lambda i: (i, 0, 0)),
        ],
        out_specs=pl.BlockSpec((tasks, span, rows, LANES), lambda i: (0, i, 0, 0)),
        out_shape=jax.ShapeDtypeStruct((tasks, dests, rows, LANES), BF16),
        scratch_shapes=[pltpu.VMEM((tasks * rows, entries), BF16)],
        cost_estimate=cost(2 * tasks * rows * entries * dests * LANES, 8 << 20),
        name="pick",
    )(ids, factors)


def sort_kernel(all_ref, row_ref, in_ref, out_ref, low_ref, part_ref, name_ref, rank_ref, slot_ref):
    step = pl.program_id(0)
    tokens = all_ref.shape[1]
    width, tile = out_ref.shape
    count = 128
    per_row = tokens // count

    @pl.when(step == 0)
    def _():
        before = one_where(iota((256, 256), 0) < iota((256, 256), 1))
        carry = jnp.zeros((count, 1), F32)
        for at in range(0, tokens, 256):
            rows = all_ref[:, at : at + 256]
            hot = jnp.where(iota((count, 256), 0) == rows, 1.0, 0.0)
            seen = product(hot.astype(BF16), before) + carry
            rank = jnp.sum(hot * seen, axis=0, keepdims=True).astype(jnp.int32)
            carry = carry + jnp.sum(hot, axis=1, keepdims=True)
            slot = rows * per_row + rank
            slot_ref[:, at : at + 256] = slot
            rank_ref[at // 256] = slot

    total = jnp.zeros((tile, width), F32)
    for at in range(0, tokens, 1024):
        place = iota((tile, 1024), 0) + step * tile
        hot = one_where(place == slot_ref[:, at : at + 1024])
        total = total + product(hot, in_ref[at : at + 1024, :])
    out_ref[...] = total.T.astype(BF16)

    for at in range(0, tile, 256):
        slot = rank_ref[step * (tile // 256) + at // 256]
        slot = jnp.broadcast_to(slot.astype(F32), (LANES, 256)).T.astype(jnp.int32)
        span = slice(at, at + 256)
        lane = iota((256, LANES), 1)
        low_ref[span, :LANES] = one_where((slot & 255) == lane)
        low_ref[span, LANES:] = one_where((slot & 255) == lane + LANES)
        part_ref[span, :] = (slot >> 8).astype(F32).astype(BF16)
        name_ref[span, :] = (slot // per_row).astype(F32).astype(BF16)


def sorted_tokens(local_row, inputs):
    tokens, width = inputs.shape
    tile = 512
    wide = lambda lanes: jax.ShapeDtypeStruct((tokens, lanes), BF16)
    return pl.pallas_call(
        sort_kernel,
        grid=(tokens // tile,),
        in_specs=[
            pl.BlockSpec((1, tokens), lambda i: (0, 0)),
            pl.BlockSpec((1, tile), lambda i: (0, i)),
            pl.BlockSpec((tokens, width), lambda i: (0, 0)),
        ],
        out_specs=[
            pl.BlockSpec((width, tile), lambda i: (0, i)),
            pl.BlockSpec((tile, 256), lambda i: (i, 0)),
            pl.BlockSpec((tile, LANES), lambda i: (i, 0)),
            pl.BlockSpec((tile, LANES), lambda i: (i, 0)),
        ],
        out_shape=[jax.ShapeDtypeStruct((width, tokens), BF16), wide(256), wide(LANES), wide(LANES)],
        scratch_shapes=[
            pltpu.VMEM((tokens // 256, 1, 256), jnp.int32),
            pltpu.VMEM((1, tokens), jnp.int32),
        ],
        cost_estimate=cost(2 * tokens * tokens * width, 16 << 20),
        name="sort",
    )(local_row, local_row, inputs)


def entry_kernel(in_ref, block_ref, out_ref):
    rows = block_ref.shape[3]
    part = 16
    slots = in_ref.shape[1] * part // rows
    match = iota((part, slots), 0) == iota((part, slots), 1) // (slots // part)
    for at in range(0, rows, part):
        span = slice(at, at + part)
        factor = jnp.concatenate(
            [block_ref[0, :, q, span].reshape(RANK * part, LANES) for q in range(4)], axis=1
        )
        first = at // part * slots
        scores = product(factor, in_ref[:, first : first + slots])
        scores = jnp.where(match[None], scores.reshape(RANK, part, slots), 0.0)
        coef = jnp.sum(scores, axis=1).astype(out_ref.dtype)
        for piece in range(0, slots, 256):
            out_ref[(first + piece) // 256] = coef[:, piece : piece + 256]


def rank_parts(inputs, blocks):
    width, tokens = inputs.shape
    rows = blocks.shape[3]
    steps = 2
    return pl.pallas_call(
        entry_kernel,
        grid=(steps,),
        in_specs=[
            pl.BlockSpec((width, tokens // steps), lambda i: (0, i)),
            pl.BlockSpec((1, RANK, 4, rows // steps, LANES), lambda i: (0, 0, 0, i, 0)),
        ],
        out_specs=pl.BlockSpec((tokens // steps // 256, RANK, 256), lambda i: (i, 0, 0)),
        out_shape=jax.ShapeDtypeStruct((tokens // 256, RANK, 256), BF16),
        name="entry",
    )(inputs, blocks)


def order_kernel(block_ref, out_ref):
    out_at = iota((256, 256), 0)
    perm = one_where(iota((256, 256), 1) == (out_at & 15) * 16 + (out_at >> 4))
    for at in range(0, block_ref.shape[3], 16):
        piece = jnp.concatenate(
            [block_ref[0, :, q, at : at + 16].reshape(RANK * 16, LANES) for q in range(4)],
            axis=1,
        )
        out_ref[at * RANK : at * RANK + 256] = product(perm, piece).astype(BF16)


def ordered_exit(blocks):
    rows = blocks.shape[3]
    part = rows // 2
    return pl.pallas_call(
        order_kernel,
        grid=(rows // part,),
        in_specs=[pl.BlockSpec((1, RANK, 4, part, LANES), lambda i: (1, 0, 0, i, 0))],
        out_specs=pl.BlockSpec((part * RANK, 4 * LANES), lambda i: (i, 0)),
        out_shape=jax.ShapeDtypeStruct((rows * RANK, 4 * LANES), BF16),
        name="order",
    )(blocks)


def exit_kernel(coef_ref, low_ref, part_ref, name_ref, base_ref, factor_ref, out_ref):
    tile = base_ref.shape[0]
    depth = factor_ref.shape[0]
    group = lane_group(tile)
    zero = jnp.zeros((tile, LANES), F32)
    values = product(low_ref[...], coef_ref[...], 1, 1)
    part = part_ref[...].astype(F32)
    group32 = group.astype(F32)
    mine = jnp.where(part == group32, values[:, :LANES], zero)
    mine = mine + jnp.where(part == group32 + 8.0, values[:, LANES:], zero)
    fold = one_where((iota((LANES, LANES), 0) & 15) == (iota((LANES, LANES), 1) & 15))
    coef = product(mine.astype(BF16), fold).astype(BF16)
    name = name_ref[...]
    spread = jnp.concatenate(
        [
            jnp.where(name == group + jnp.asarray(at, BF16), coef, jnp.zeros_like(coef))
            for at in range(0, depth // RANK, 8)
        ],
        axis=1,
    )
    update = product(spread, factor_ref[...])
    base = base_ref[...].astype(F32)
    out_ref[...] = (base + update * (1.0 / math.sqrt(RANK))).astype(BF16)


def apply_update(coefs, low, part, name, base, factors):
    tokens, width = base.shape
    tile = 1024
    return pl.pallas_call(
        exit_kernel,
        grid=(tokens // tile,),
        in_specs=[
            pl.BlockSpec(coefs.shape, lambda i: (0, 0)),
            pl.BlockSpec((tile, 256), lambda i: (i, 0)),
            pl.BlockSpec((tile, LANES), lambda i: (i, 0)),
            pl.BlockSpec((tile, LANES), lambda i: (i, 0)),
            pl.BlockSpec((tile, width), lambda i: (i, 0)),
            pl.BlockSpec(factors.shape, lambda i: (0, 0)),
        ],
        out_specs=pl.BlockSpec((tile, width), lambda i: (i, 0)),
        out_shape=jax.ShapeDtypeStruct((tokens, width), BF16),
        name="exit",
    )(coefs, low, part, name, base, factors)


def to_all(shard, axis):
    length = lax.axis_size(axis)
    return lax.all_to_all(
        jnp.broadcast_to(shard[None], (length, *shard.shape)), axis, 0, 0, tiled=True
    )


def on_device(
    task_ids,
    embed_table,
    trunk_weight,
    trunk_bias,
    head_weight,
    head_bias,
    token_row,
    inputs,
    frozen,
):
    tasks = lax.axis_size("task")
    width = lax.axis_size("width")
    rows_dev = task_ids.shape[0]
    me = lax.axis_index("task")
    ids = to_all(task_ids, "task").reshape(tasks, rows_dev)
    factors = table_factors(
        embed_table,
        trunk_weight,
        trunk_bias.reshape(1, -1),
        head_weight,
        head_bias.reshape(1, -1),
    )
    blocks = picked_rows(ids, factors)
    moved = lax.all_to_all(
        blocks.reshape(tasks * width, rows_dev, LANES), BOTH, 0, 0, tiled=True
    ).reshape(2, RANK, 4, rows_dev, LANES)

    local_row = (token_row - me * rows_dev).reshape(1, -1)
    in_order, low, part, name = sorted_tokens(local_row, inputs)
    parts = rank_parts(in_order, moved)
    pieces = lax.all_to_all(parts, "width", 0, 0, tiled=True).astype(F32)
    coef = (pieces.sum(axis=0) * (1.0 / math.sqrt(WIDTH))).astype(BF16)
    coefs = to_all(coef, "width").reshape(width * RANK, -1)
    return apply_update(coefs, low, part, name, frozen, ordered_exit(moved))


def solution(mesh):
    return jax.shard_map(
        on_device,
        mesh=mesh,
        in_specs=(
            P("task"),
            P(),
            P(),
            P(),
            P(None, BOTH),
            P(BOTH),
            P("task"),
            P("task", "width"),
            P("task", "width"),
        ),
        out_specs=P("task", "width"),
        check_vma=False,
    )
```

```python
import math

import jax
import jax.numpy as jnp
from jax import lax
from jax.experimental import pallas as pl
from jax.experimental.pallas import tpu as pltpu
from jax.sharding import PartitionSpec as P

WIDTH = 8192
RANK = 16
LANES = 128
BOTH = ("task", "width")
BF16 = jnp.bfloat16
F32 = jnp.float32
HELD = pl.BlockSpec(memory_space=pltpu.VMEM)
ROOM = pltpu.CompilerParams(vmem_limit_bytes=40 << 20)


def product(a, b, a_dim=1, b_dim=0):
    return lax.dot_general(a, b, (((a_dim,), (b_dim,)), ((), ())), preferred_element_type=F32)


def iota(shape, dim):
    return lax.broadcasted_iota(jnp.int32, shape, dim)


def one_where(test):
    return jnp.where(test, 1.0, 0.0).astype(BF16)


def lane_group(rows):
    return (iota((rows, LANES), 1) >> 4).astype(F32).astype(BF16)


def cost(flops, moved):
    return pl.CostEstimate(flops=int(flops), transcendentals=0, bytes_accessed=int(moved))


def table_kernel(
    embed_ref, trunk_ref, trunk_bias_ref, weight_ref, bias_ref, out_ref, hidden_ref
):
    step = pl.program_id(0)
    hid = hidden_ref.shape[1]
    wide = 512
    early = hid // wide

    @pl.when(step < early)
    def _():
        span = pl.ds(pl.multiple_of(step * wide, wide), wide)
        value = product(embed_ref[...], trunk_ref[...]) + trunk_bias_ref[...]
        hidden_ref[:, span] = jax.nn.silu(value).astype(BF16)

    @pl.when(step >= early)
    def _():
        block = step - early
        out = product(hidden_ref[...], weight_ref[...]) + bias_ref[...]
        col = iota((256, 256), 0)
        target = ((col >> 3) & 1) * 128 + ((block + col) & 7) * 16 + (col >> 4)
        perm = one_where(iota((256, 256), 1) == target)
        out_ref[0] = product(out.astype(BF16), perm).astype(BF16)


def table_factors(embed, trunk, trunk_bias, head_weight, bias):
    entries, width = embed.shape
    hid, cols = head_weight.shape
    early, blocks = hid // 512, cols // 256
    first = lambda i: (0, jnp.minimum(i, early - 1))
    then = lambda i: (0, jnp.maximum(i - early, 0))
    return pl.pallas_call(
        table_kernel,
        grid=(early + blocks,),
        in_specs=[
            pl.BlockSpec(embed.shape, lambda i: (0, 0)),
            pl.BlockSpec((width, 512), first),
            pl.BlockSpec((1, 512), first),
            pl.BlockSpec((hid, 256), then),
            pl.BlockSpec((1, 256), then),
        ],
        out_specs=pl.BlockSpec(
            (1, entries, 256), lambda i: (jnp.maximum(i - early, 0), 0, 0)
        ),
        out_shape=jax.ShapeDtypeStruct((blocks, entries, 256), BF16),
        scratch_shapes=[pltpu.VMEM((entries, hid), BF16)],
        cost_estimate=cost(2 * entries * hid * (width + cols), 18 << 20),
        name="table",
    )(embed, trunk, trunk_bias, head_weight, bias)


def pick_kernel(id_ref, table_ref, out_ref, hot_ref, mixed_ref):
    tasks, rows = id_ref.shape
    blocks, entries, _ = table_ref.shape
    half = pl.program_id(0)

    @pl.when(half == 0)
    def _():
        lane = iota((rows, LANES), 1).astype(F32)
        for task in range(tasks):
            ids = jnp.broadcast_to(id_ref[task : task + 1, :].astype(F32), (LANES, rows)).T
            for at in range(0, entries, LANES):
                hot_ref[task * rows : (task + 1) * rows, at : at + LANES] = one_where(
                    ids == lane + float(at)
                )

    group = lane_group(entries)

    def mix(first):
        for turn in (first, first + 1):
            mixed = table_ref[0]
            for block in range(1, blocks):
                place = jnp.asarray((block + turn) % 8, BF16)
                mixed = jnp.where(group == place, table_ref[block], mixed)
            mixed_ref[:, turn * LANES : (turn + 1) * LANES] = mixed

    mix(0)
    for first in range(0, 8, 2):
        if first + 2 < 8:
            mix(first + 2)
        picked = product(hot_ref[...], mixed_ref[:, first * LANES : (first + 2) * LANES])
        for side in range(2):
            turn = first + side
            piece = picked[:, side * LANES : side * LANES + LANES]
            if turn:
                piece = pltpu.roll(piece, LANES - 16 * turn, 1)
            out_ref[:, turn] = piece.astype(BF16).reshape(tasks, rows, LANES)


def picked_rows(ids, factors):
    tasks, rows = ids.shape
    blocks, entries, _ = factors.shape
    return pl.pallas_call(
        pick_kernel,
        grid=(2,),
        in_specs=[HELD, pl.BlockSpec((blocks, entries, LANES), lambda i: (0, 0, i))],
        out_specs=pl.BlockSpec((tasks, 8, rows, LANES), lambda i: (0, i, 0, 0)),
        out_shape=jax.ShapeDtypeStruct((tasks, 16, rows, LANES), BF16),
        scratch_shapes=[
            pltpu.VMEM((tasks * rows, entries), BF16),
            pltpu.VMEM((entries, 8 * LANES), BF16),
        ],
        cost_estimate=cost(2 * tasks * rows * entries * 16 * LANES, 8 << 20),
        name="pick",
    )(ids, factors)


def sort_kernel(all_ref, row_ref, in_ref, out_ref, low_ref, part_ref, name_ref, rank_ref, slot_ref):
    step = pl.program_id(0)
    tokens = all_ref.shape[1]
    width, tile = out_ref.shape
    count = 128
    per_row = tokens // count

    @pl.when(step == 0)
    def _():
        before = one_where(iota((256, 256), 0) < iota((256, 256), 1))
        carry = jnp.zeros((count, 1), F32)
        for at in range(0, tokens, 256):
            rows = all_ref[:, at : at + 256]
            hot = jnp.where(iota((count, 256), 0) == rows, 1.0, 0.0)
            seen = product(hot.astype(BF16), before) + carry
            rank = jnp.sum(hot * seen, axis=0, keepdims=True).astype(jnp.int32)
            carry = carry + jnp.sum(hot, axis=1, keepdims=True)
            slot = rows * per_row + rank
            slot_ref[:, at : at + 256] = slot
            rank_ref[at // 256] = slot

    total = jnp.zeros((tile, width), F32)
    for at in range(0, tokens, 1024):
        place = iota((tile, 1024), 0) + step * tile
        hot = one_where(place == slot_ref[:, at : at + 1024])
        total = total + product(hot, in_ref[at : at + 1024, :])
    out_ref[...] = total.T.astype(BF16)

    for at in range(0, tile, 256):
        slot = rank_ref[step * (tile // 256) + at // 256]
        slot = jnp.broadcast_to(slot.astype(F32), (LANES, 256)).T.astype(jnp.int32)
        span = slice(at, at + 256)
        lane = iota((256, LANES), 1)
        low_ref[span, :LANES] = one_where((slot & 255) == lane)
        low_ref[span, LANES:] = one_where((slot & 255) == lane + LANES)
        part_ref[span, :] = (slot >> 8).astype(F32).astype(BF16)
        name_ref[span, :] = (slot // per_row).astype(F32).astype(BF16)


def sorted_tokens(local_row, inputs):
    tokens, width = inputs.shape
    tile = 512
    wide = lambda lanes: jax.ShapeDtypeStruct((tokens, lanes), BF16)
    return pl.pallas_call(
        sort_kernel,
        grid=(tokens // tile,),
        in_specs=[
            pl.BlockSpec((1, tokens), lambda i: (0, 0)),
            pl.BlockSpec((1, tile), lambda i: (0, i)),
            pl.BlockSpec((tokens, width), lambda i: (0, 0)),
        ],
        out_specs=[
            pl.BlockSpec((width, tile), lambda i: (0, i)),
            pl.BlockSpec((tile, 256), lambda i: (i, 0)),
            pl.BlockSpec((tile, LANES), lambda i: (i, 0)),
            pl.BlockSpec((tile, LANES), lambda i: (i, 0)),
        ],
        out_shape=[jax.ShapeDtypeStruct((width, tokens), BF16), wide(256), wide(LANES), wide(LANES)],
        scratch_shapes=[
            pltpu.VMEM((tokens // 256, 1, 256), jnp.int32),
            pltpu.VMEM((1, tokens), jnp.int32),
        ],
        cost_estimate=cost(2 * tokens * tokens * width, 16 << 20),
        name="sort",
    )(local_row, local_row, inputs)


def entry_kernel(in_ref, block_ref, out_ref):
    rows = block_ref.shape[3]
    part = 16
    slots = in_ref.shape[1] * part // rows
    match = iota((part, slots), 0) == iota((part, slots), 1) // (slots // part)
    for at in range(0, rows, part):
        span = slice(at, at + part)
        factor = jnp.concatenate(
            [block_ref[0, :, q, span].reshape(RANK * part, LANES) for q in range(4)], axis=1
        )
        first = at // part * slots
        scores = product(factor, in_ref[:, first : first + slots])
        scores = jnp.where(match[None], scores.reshape(RANK, part, slots), 0.0)
        coef = jnp.sum(scores, axis=1).astype(out_ref.dtype)
        for piece in range(0, slots, 256):
            out_ref[(first + piece) // 256] = coef[:, piece : piece + 256]


def rank_parts(inputs, blocks):
    width, tokens = inputs.shape
    rows = blocks.shape[3]
    steps = 2
    return pl.pallas_call(
        entry_kernel,
        grid=(steps,),
        in_specs=[
            pl.BlockSpec((width, tokens // steps), lambda i: (0, i)),
            pl.BlockSpec((1, RANK, 4, rows // steps, LANES), lambda i: (0, 0, 0, i, 0)),
        ],
        out_specs=pl.BlockSpec((tokens // steps // 256, RANK, 256), lambda i: (i, 0, 0)),
        out_shape=jax.ShapeDtypeStruct((tokens // 256, RANK, 256), BF16),
        name="entry",
    )(inputs, blocks)


def order_kernel(block_ref, out_ref):
    out_at = iota((256, 256), 0)
    perm = one_where(iota((256, 256), 1) == (out_at & 15) * 16 + (out_at >> 4))
    for at in range(0, block_ref.shape[3], 16):
        piece = jnp.concatenate(
            [block_ref[0, :, q, at : at + 16].reshape(RANK * 16, LANES) for q in range(4)],
            axis=1,
        )
        out_ref[at * RANK : at * RANK + 256] = product(perm, piece).astype(BF16)


def ordered_exit(blocks):
    rows = blocks.shape[3]
    part = rows // 2
    return pl.pallas_call(
        order_kernel,
        grid=(rows // part,),
        in_specs=[pl.BlockSpec((1, RANK, 4, part, LANES), lambda i: (1, 0, 0, i, 0))],
        out_specs=pl.BlockSpec((part * RANK, 4 * LANES), lambda i: (i, 0)),
        out_shape=jax.ShapeDtypeStruct((rows * RANK, 4 * LANES), BF16),
        compiler_params=ROOM,
        name="order",
    )(blocks)


def exit_kernel(coef_ref, low_ref, part_ref, name_ref, base_ref, factor_ref, out_ref):
    tile = base_ref.shape[0]
    depth = factor_ref.shape[0]
    group = lane_group(tile)
    zero = jnp.zeros((tile, LANES), F32)
    values = product(low_ref[...], coef_ref[...].reshape(256, 256), 1, 1)
    part = part_ref[...].astype(F32)
    group32 = group.astype(F32)
    mine = jnp.where(part == group32, values[:, :LANES], zero)
    mine = mine + jnp.where(part == group32 + 8.0, values[:, LANES:], zero)
    fold = one_where((iota((LANES, LANES), 0) & 15) == (iota((LANES, LANES), 1) & 15))
    coef = product(mine.astype(BF16), fold).astype(BF16)
    name = name_ref[...]
    spread = jnp.concatenate(
        [
            jnp.where(name == group + jnp.asarray(at, BF16), coef, jnp.zeros_like(coef))
            for at in range(0, depth // RANK, 8)
        ],
        axis=1,
    )
    update = product(spread, factor_ref[...])
    base = base_ref[...].astype(F32)
    out_ref[...] = (base + update * (1.0 / math.sqrt(RANK))).astype(BF16)


def apply_update(coefs, low, part, name, base, factors):
    tokens, width = base.shape
    tile = 1024
    low, part, name, base = (
        pltpu.with_memory_space_constraint(array, pltpu.MemorySpace.HBM)
        for array in (low, part, name, base)
    )
    return pl.pallas_call(
        exit_kernel,
        grid=(tokens // tile,),
        in_specs=[
            HELD,
            pl.BlockSpec((tile, 256), lambda i: (i, 0)),
            pl.BlockSpec((tile, LANES), lambda i: (i, 0)),
            pl.BlockSpec((tile, LANES), lambda i: (i, 0)),
            pl.BlockSpec((tile, width), lambda i: (i, 0)),
            HELD,
        ],
        out_specs=pl.BlockSpec((tile, width), lambda i: (i, 0)),
        out_shape=jax.ShapeDtypeStruct((tokens, width), BF16),
        compiler_params=ROOM,
        name="exit",
    )(coefs, low, part, name, base, factors)


def to_all(shard, axis):
    length = lax.axis_size(axis)
    return lax.all_to_all(
        jnp.broadcast_to(shard[None], (length, *shard.shape)), axis, 0, 0, tiled=True
    )


def on_device(
    task_ids,
    embed_table,
    trunk_weight,
    trunk_bias,
    head_weight,
    head_bias,
    token_row,
    inputs,
    frozen,
):
    tasks = lax.axis_size("task")
    width = lax.axis_size("width")
    rows_dev = task_ids.shape[0]
    me = lax.axis_index("task")
    ids = to_all(task_ids, "task").reshape(tasks, rows_dev)
    factors = table_factors(
        embed_table,
        trunk_weight,
        trunk_bias.reshape(1, -1),
        head_weight,
        head_bias.reshape(1, -1),
    )
    blocks = picked_rows(ids, factors)
    moved = lax.all_to_all(
        blocks.reshape(tasks * width, rows_dev, LANES), BOTH, 0, 0, tiled=True
    ).reshape(2, RANK, 4, rows_dev, LANES)

    local_row = (token_row - me * rows_dev).reshape(1, -1)
    in_order, low, part, name = sorted_tokens(local_row, inputs)
    parts = rank_parts(in_order, moved)
    pieces = lax.all_to_all(parts, "width", 0, 0, tiled=True).astype(F32)
    coef = (pieces.sum(axis=0) * (1.0 / math.sqrt(WIDTH))).astype(BF16)
    coefs = to_all(coef, "width")
    return apply_update(coefs, low, part, name, frozen, ordered_exit(moved))


def solution(mesh):
    return jax.shard_map(
        on_device,
        mesh=mesh,
        in_specs=(
            P("task"),
            P(),
            P(),
            P(),
            P(None, BOTH),
            P(BOTH),
            P("task"),
            P("task", "width"),
            P("task", "width"),
        ),
        out_specs=P("task", "width"),
        check_vma=False,
    )
```

```python
import math

import jax
import jax.numpy as jnp
from jax import lax
from jax.experimental import pallas as pl
from jax.experimental.pallas import tpu as pltpu
from jax.sharding import PartitionSpec as P

WIDTH = 8192
RANK = 16
LANES = 128
BOTH = ("task", "width")
BF16 = jnp.bfloat16
F32 = jnp.float32
HELD = pl.BlockSpec(memory_space=pltpu.VMEM)
ROOM = pltpu.CompilerParams(vmem_limit_bytes=40 << 20)


def product(a, b, a_dim=1, b_dim=0):
    return lax.dot_general(a, b, (((a_dim,), (b_dim,)), ((), ())), preferred_element_type=F32)


def iota(shape, dim):
    return lax.broadcasted_iota(jnp.int32, shape, dim)


def one_where(test):
    return jnp.where(test, 1.0, 0.0).astype(BF16)


def lane_group(rows):
    return (iota((rows, LANES), 1) >> 4).astype(F32).astype(BF16)


def cost(flops, moved):
    return pl.CostEstimate(flops=int(flops), transcendentals=0, bytes_accessed=int(moved))


def table_kernel(
    embed_ref, trunk_ref, trunk_bias_ref, weight_ref, bias_ref, out_ref, hidden_ref
):
    step = pl.program_id(0)
    hid = hidden_ref.shape[1]
    wide = 512
    early = hid // wide

    @pl.when(step < early)
    def _():
        span = pl.ds(pl.multiple_of(step * wide, wide), wide)
        value = product(embed_ref[...], trunk_ref[...]) + trunk_bias_ref[...]
        hidden_ref[:, span] = jax.nn.silu(value).astype(BF16)

    @pl.when(step >= early)
    def _():
        block = step - early
        out = product(hidden_ref[...], weight_ref[...]) + bias_ref[...]
        col = iota((256, 256), 0)
        target = ((col >> 3) & 1) * 128 + ((block + col) & 7) * 16 + (col >> 4)
        perm = one_where(iota((256, 256), 1) == target)
        out_ref[0] = product(out.astype(BF16), perm).astype(BF16)


def table_factors(embed, trunk, trunk_bias, head_weight, bias):
    entries, width = embed.shape
    hid, cols = head_weight.shape
    early, blocks = hid // 512, cols // 256
    first = lambda i: (0, jnp.minimum(i, early - 1))
    then = lambda i: (0, jnp.maximum(i - early, 0))
    return pl.pallas_call(
        table_kernel,
        grid=(early + blocks,),
        in_specs=[
            pl.BlockSpec(embed.shape, lambda i: (0, 0)),
            pl.BlockSpec((width, 512), first),
            pl.BlockSpec((1, 512), first),
            pl.BlockSpec((hid, 256), then),
            pl.BlockSpec((1, 256), then),
        ],
        out_specs=pl.BlockSpec(
            (1, entries, 256), lambda i: (jnp.maximum(i - early, 0), 0, 0)
        ),
        out_shape=jax.ShapeDtypeStruct((blocks, entries, 256), BF16),
        scratch_shapes=[pltpu.VMEM((entries, hid), BF16)],
        cost_estimate=cost(2 * entries * hid * (width + cols), 18 << 20),
        name="table",
    )(embed, trunk, trunk_bias, head_weight, bias)


def pick_kernel(id_ref, table_ref, out_ref, hot_ref, mixed_ref):
    tasks, _, rows = id_ref.shape
    blocks, entries, _ = table_ref.shape
    half = pl.program_id(0)

    @pl.when(half == 0)
    def _():
        lane = iota((rows, LANES), 1).astype(F32)
        for task in range(tasks):
            ids = jnp.broadcast_to(id_ref[task, :1].astype(F32), (LANES, rows)).T
            for at in range(0, entries, LANES):
                hot_ref[task * rows : (task + 1) * rows, at : at + LANES] = one_where(
                    ids == lane + float(at)
                )

    group = lane_group(entries)

    def mix(first):
        for turn in (first, first + 1):
            mixed = table_ref[0]
            for block in range(1, blocks):
                place = jnp.asarray((block + turn) % 8, BF16)
                mixed = jnp.where(group == place, table_ref[block], mixed)
            mixed_ref[:, turn * LANES : (turn + 1) * LANES] = mixed

    mix(0)
    for first in range(0, 8, 2):
        if first + 2 < 8:
            mix(first + 2)
        picked = product(hot_ref[...], mixed_ref[:, first * LANES : (first + 2) * LANES])
        for side in range(2):
            turn = first + side
            piece = picked[:, side * LANES : side * LANES + LANES]
            if turn:
                piece = pltpu.roll(piece, LANES - 16 * turn, 1)
            out_ref[:, turn] = piece.astype(BF16).reshape(tasks, rows, LANES)


def picked_rows(ids, factors):
    tasks, _, rows = ids.shape
    blocks, entries, _ = factors.shape
    ids = pltpu.with_memory_space_constraint(ids, pltpu.MemorySpace.HBM)
    return pl.pallas_call(
        pick_kernel,
        grid=(2,),
        in_specs=[
            pl.BlockSpec(ids.shape, lambda i: (0, 0, 0)),
            pl.BlockSpec((blocks, entries, LANES), lambda i: (0, 0, i)),
        ],
        out_specs=pl.BlockSpec((tasks, 8, rows, LANES), lambda i: (0, i, 0, 0)),
        out_shape=jax.ShapeDtypeStruct((tasks, 16, rows, LANES), BF16),
        scratch_shapes=[
            pltpu.VMEM((tasks * rows, entries), BF16),
            pltpu.VMEM((entries, 8 * LANES), BF16),
        ],
        cost_estimate=cost(2 * tasks * rows * entries * 16 * LANES, 8 << 20),
        name="pick",
    )(ids, factors)


def sort_kernel(all_ref, row_ref, in_ref, out_ref, low_ref, part_ref, name_ref, rank_ref, slot_ref):
    step = pl.program_id(0)
    tokens = all_ref.shape[1]
    width, tile = out_ref.shape
    count = 128
    per_row = tokens // count

    @pl.when(step == 0)
    def _():
        before = one_where(iota((256, 256), 0) < iota((256, 256), 1))
        carry = jnp.zeros((count, 1), F32)
        for at in range(0, tokens, 256):
            rows = all_ref[:, at : at + 256]
            hot = jnp.where(iota((count, 256), 0) == rows, 1.0, 0.0)
            seen = product(hot.astype(BF16), before) + carry
            rank = jnp.sum(hot * seen, axis=0, keepdims=True).astype(jnp.int32)
            carry = carry + jnp.sum(hot, axis=1, keepdims=True)
            slot = rows * per_row + rank
            slot_ref[:, at : at + 256] = slot
            rank_ref[at // 256] = slot

    total = jnp.zeros((tile, width), F32)
    for at in range(0, tokens, 1024):
        place = iota((tile, 1024), 0) + step * tile
        hot = one_where(place == slot_ref[:, at : at + 1024])
        total = total + product(hot, in_ref[at : at + 1024, :])
    out_ref[...] = total.T.astype(BF16)

    for at in range(0, tile, 256):
        slot = rank_ref[step * (tile // 256) + at // 256]
        slot = jnp.broadcast_to(slot.astype(F32), (LANES, 256)).T.astype(jnp.int32)
        span = slice(at, at + 256)
        lane = iota((256, LANES), 1)
        low_ref[span, :LANES] = one_where((slot & 255) == lane)
        low_ref[span, LANES:] = one_where((slot & 255) == lane + LANES)
        part_ref[span, :] = (slot >> 8).astype(F32).astype(BF16)
        name_ref[span, :] = (slot // per_row).astype(F32).astype(BF16)


def sorted_tokens(local_row, inputs):
    tokens, width = inputs.shape
    tile = 512
    wide = lambda lanes: jax.ShapeDtypeStruct((tokens, lanes), BF16)
    return pl.pallas_call(
        sort_kernel,
        grid=(tokens // tile,),
        in_specs=[
            pl.BlockSpec((1, tokens), lambda i: (0, 0)),
            pl.BlockSpec((1, tile), lambda i: (0, i)),
            pl.BlockSpec((tokens, width), lambda i: (0, 0)),
        ],
        out_specs=[
            pl.BlockSpec((width, tile), lambda i: (0, i)),
            pl.BlockSpec((tile, 256), lambda i: (i, 0)),
            pl.BlockSpec((tile, LANES), lambda i: (i, 0)),
            pl.BlockSpec((tile, LANES), lambda i: (i, 0)),
        ],
        out_shape=[jax.ShapeDtypeStruct((width, tokens), BF16), wide(256), wide(LANES), wide(LANES)],
        scratch_shapes=[
            pltpu.VMEM((tokens // 256, 1, 256), jnp.int32),
            pltpu.VMEM((1, tokens), jnp.int32),
        ],
        cost_estimate=cost(2 * tokens * tokens * width, 16 << 20),
        name="sort",
    )(local_row, local_row, inputs)


def entry_kernel(in_ref, block_ref, out_ref):
    rows = block_ref.shape[3]
    part = 16
    slots = in_ref.shape[1] * part // rows
    match = iota((part, slots), 0) == iota((part, slots), 1) // (slots // part)
    for at in range(0, rows, part):
        span = slice(at, at + part)
        factor = jnp.concatenate(
            [block_ref[0, :, q, span].reshape(RANK * part, LANES) for q in range(4)], axis=1
        )
        first = at // part * slots
        scores = product(factor, in_ref[:, first : first + slots])
        scores = jnp.where(match[None], scores.reshape(RANK, part, slots), 0.0)
        coef = jnp.sum(scores, axis=1).astype(out_ref.dtype)
        for piece in range(0, slots, 256):
            out_ref[(first + piece) // 256] = coef[:, piece : piece + 256]


def rank_parts(inputs, blocks):
    width, tokens = inputs.shape
    rows = blocks.shape[3]
    steps = 2
    return pl.pallas_call(
        entry_kernel,
        grid=(steps,),
        in_specs=[
            pl.BlockSpec((width, tokens // steps), lambda i: (0, i)),
            pl.BlockSpec((1, RANK, 4, rows // steps, LANES), lambda i: (0, 0, 0, i, 0)),
        ],
        out_specs=pl.BlockSpec((tokens // steps // 256, RANK, 256), lambda i: (i, 0, 0)),
        out_shape=jax.ShapeDtypeStruct((tokens // 256, RANK, 256), BF16),
        name="entry",
    )(inputs, blocks)


def order_kernel(block_ref, out_ref):
    out_at = iota((256, 256), 0)
    perm = one_where(iota((256, 256), 1) == (out_at & 15) * 16 + (out_at >> 4))
    for at in range(0, block_ref.shape[3], 16):
        piece = jnp.concatenate(
            [block_ref[0, :, q, at : at + 16].reshape(RANK * 16, LANES) for q in range(4)],
            axis=1,
        )
        out_ref[at * RANK : at * RANK + 256] = product(perm, piece).astype(BF16)


def ordered_exit(blocks):
    rows = blocks.shape[3]
    part = rows // 2
    return pl.pallas_call(
        order_kernel,
        grid=(rows // part,),
        in_specs=[pl.BlockSpec((1, RANK, 4, part, LANES), lambda i: (1, 0, 0, i, 0))],
        out_specs=pl.BlockSpec((part * RANK, 4 * LANES), lambda i: (i, 0)),
        out_shape=jax.ShapeDtypeStruct((rows * RANK, 4 * LANES), BF16),
        compiler_params=ROOM,
        name="order",
    )(blocks)


def exit_kernel(coef_ref, low_ref, part_ref, name_ref, base_ref, factor_ref, out_ref):
    tile = base_ref.shape[0]
    depth = factor_ref.shape[0]
    group = lane_group(tile)
    zero = jnp.zeros((tile, LANES), F32)
    values = product(low_ref[...], coef_ref[...].reshape(256, 256), 1, 1)
    part = part_ref[...].astype(F32)
    group32 = group.astype(F32)
    mine = jnp.where(part == group32, values[:, :LANES], zero)
    mine = mine + jnp.where(part == group32 + 8.0, values[:, LANES:], zero)
    fold = one_where((iota((LANES, LANES), 0) & 15) == (iota((LANES, LANES), 1) & 15))
    coef = product(mine.astype(BF16), fold).astype(BF16)
    name = name_ref[...]
    spread = jnp.concatenate(
        [
            jnp.where(name == group + jnp.asarray(at, BF16), coef, jnp.zeros_like(coef))
            for at in range(0, depth // RANK, 8)
        ],
        axis=1,
    )
    update = product(spread, factor_ref[...])
    base = base_ref[...].astype(F32)
    out_ref[...] = (base + update * (1.0 / math.sqrt(RANK))).astype(BF16)


def apply_update(coefs, low, part, name, base, factors):
    tokens, width = base.shape
    tile = 1024
    low, part, name, base = (
        pltpu.with_memory_space_constraint(array, pltpu.MemorySpace.HBM)
        for array in (low, part, name, base)
    )
    return pl.pallas_call(
        exit_kernel,
        grid=(tokens // tile,),
        in_specs=[
            HELD,
            pl.BlockSpec((tile, 256), lambda i: (i, 0)),
            pl.BlockSpec((tile, LANES), lambda i: (i, 0)),
            pl.BlockSpec((tile, LANES), lambda i: (i, 0)),
            pl.BlockSpec((tile, width), lambda i: (i, 0)),
            HELD,
        ],
        out_specs=pl.BlockSpec((tile, width), lambda i: (i, 0)),
        out_shape=jax.ShapeDtypeStruct((tokens, width), BF16),
        compiler_params=ROOM,
        name="exit",
    )(coefs, low, part, name, base, factors)


def to_all(shard, axis):
    length = lax.axis_size(axis)
    return lax.all_to_all(
        jnp.broadcast_to(shard[None], (length, *shard.shape)), axis, 0, 0, tiled=True
    )


def on_device(
    task_ids,
    embed_table,
    trunk_weight,
    trunk_bias,
    head_weight,
    head_bias,
    token_row,
    inputs,
    frozen,
):
    tasks = lax.axis_size("task")
    width = lax.axis_size("width")
    rows_dev = task_ids.shape[0]
    me = lax.axis_index("task")
    ids = to_all(task_ids, BOTH).reshape(tasks, width, rows_dev)
    factors = table_factors(
        embed_table,
        trunk_weight,
        trunk_bias.reshape(1, -1),
        head_weight,
        head_bias.reshape(1, -1),
    )
    blocks = picked_rows(ids, factors)
    moved = lax.all_to_all(
        blocks.reshape(tasks * width, rows_dev, LANES), BOTH, 0, 0, tiled=True
    ).reshape(2, RANK, 4, rows_dev, LANES)

    local_row = (token_row - me * rows_dev).reshape(1, -1)
    in_order, low, part, name = sorted_tokens(local_row, inputs)
    parts = rank_parts(in_order, moved)
    pieces = lax.all_to_all(parts, "width", 0, 0, tiled=True).astype(F32)
    coef = (pieces.sum(axis=0) * (1.0 / math.sqrt(WIDTH))).astype(BF16)
    coefs = to_all(coef, "width")
    return apply_update(coefs, low, part, name, frozen, ordered_exit(moved))


def solution(mesh):
    return jax.shard_map(
        on_device,
        mesh=mesh,
        in_specs=(
            P("task"),
            P(),
            P(),
            P(),
            P(None, BOTH),
            P(BOTH),
            P("task"),
            P("task", "width"),
            P("task", "width"),
        ),
        out_specs=P("task", "width"),
        check_vma=False,
    )
```

```python
import math

import jax
import jax.numpy as jnp
from jax import lax
from jax.experimental import pallas as pl
from jax.experimental.pallas import tpu as pltpu
from jax.sharding import PartitionSpec as P

WIDTH = 8192
RANK = 16
LANES = 128
BOTH = ("task", "width")
BF16 = jnp.bfloat16
F32 = jnp.float32
HBM = pl.BlockSpec(memory_space=pltpu.MemorySpace.HBM)
HELD = pl.BlockSpec(memory_space=pltpu.VMEM)
ROOM = pltpu.CompilerParams(vmem_limit_bytes=40 << 20)


def product(a, b, a_dim=1, b_dim=0):
    return lax.dot_general(a, b, (((a_dim,), (b_dim,)), ((), ())), preferred_element_type=F32)


def iota(shape, dim):
    return lax.broadcasted_iota(jnp.int32, shape, dim)


def one_where(test):
    return jnp.where(test, 1.0, 0.0).astype(BF16)


def lane_group(rows):
    return (iota((rows, LANES), 1) >> 4).astype(F32).astype(BF16)


def cost(flops, moved):
    return pl.CostEstimate(flops=int(flops), transcendentals=0, bytes_accessed=int(moved))


def table_kernel(
    embed_ref, trunk_ref, trunk_bias_ref, weight_ref, bias_ref, out_ref, hidden_ref
):
    step = pl.program_id(0)
    hid = hidden_ref.shape[1]
    wide = trunk_ref.shape[1]
    early = hid // wide

    @pl.when(step < early)
    def _():
        span = pl.ds(pl.multiple_of(step * wide, wide), wide)
        value = product(embed_ref[...], trunk_ref[...]) + trunk_bias_ref[...]
        hidden_ref[:, span] = jax.nn.silu(value).astype(BF16)

    @pl.when(step >= early)
    def _():
        block = step - early
        out = product(hidden_ref[...], weight_ref[...]) + bias_ref[...]
        col = iota((256, 256), 0)
        target = ((col >> 3) & 1) * 128 + ((block + col) & 7) * 16 + (col >> 4)
        perm = one_where(iota((256, 256), 1) == target)
        out_ref[0] = product(out.astype(BF16), perm).astype(BF16)


def table_factors(embed, trunk, trunk_bias, head_weight, bias):
    entries, width = embed.shape
    hid, cols = head_weight.shape
    early, blocks = hid // 1024, cols // 256
    first = lambda i: (0, jnp.minimum(i, early - 1))
    then = lambda i: (0, jnp.maximum(i - early, 0))
    return pl.pallas_call(
        table_kernel,
        grid=(early + blocks,),
        in_specs=[
            pl.BlockSpec(embed.shape, lambda i: (0, 0)),
            pl.BlockSpec((width, 1024), first),
            pl.BlockSpec((1, 1024), first),
            pl.BlockSpec((hid, 256), then),
            pl.BlockSpec((1, 256), then),
        ],
        out_specs=pl.BlockSpec(
            (1, entries, 256), lambda i: (jnp.maximum(i - early, 0), 0, 0)
        ),
        out_shape=jax.ShapeDtypeStruct((blocks, entries, 256), BF16),
        scratch_shapes=[pltpu.VMEM((entries, hid), BF16)],
        cost_estimate=cost(2 * entries * hid * (width + cols), 18 << 20),
        name="table",
    )(embed, trunk, trunk_bias, head_weight, bias)


def pick_kernel(id_ref, table_ref, out_ref, hot_ref, tile_ref, mixed_ref, sent_ref, in_sem, out_sem):
    tasks, rows = id_ref.shape
    blocks, entries, _ = table_ref.shape
    loads = []
    for half in range(2):
        lanes = pl.ds(half * LANES, LANES)
        loads.append(
            pltpu.make_async_copy(
                table_ref.at[:, :, lanes], tile_ref.at[half], in_sem.at[half]
            )
        )
        loads[half].start()
    lane = iota((rows, LANES), 1).astype(F32)
    for task in range(tasks):
        ids = jnp.broadcast_to(id_ref[task : task + 1, :].astype(F32), (LANES, rows)).T
        for at in range(0, entries, LANES):
            hot_ref[task * rows : (task + 1) * rows, at : at + LANES] = one_where(
                ids == lane + float(at)
            )
    group = lane_group(entries)

    def mix(pair):
        half, first = pair // 4, pair % 4 * 2
        if first == 0:
            loads[half].wait()
        for side in range(2):
            mixed = tile_ref[half, 0]
            for block in range(1, blocks):
                place = jnp.asarray((block + first + side) % 8, BF16)
                mixed = jnp.where(group == place, tile_ref[half, block], mixed)
            mixed_ref[pair % 2, :, side * LANES : (side + 1) * LANES] = mixed

    mix(0)
    stores = []
    for pair in range(8):
        if pair + 1 < 8:
            mix(pair + 1)
        picked = product(hot_ref[...], mixed_ref[pair % 2])
        for side in range(2):
            turn = pair % 4 * 2 + side
            piece = picked[:, side * LANES : side * LANES + LANES]
            if turn:
                piece = pltpu.roll(piece, LANES - 16 * turn, 1)
            sent_ref[:, 2 * pair + side] = piece.astype(BF16).reshape(tasks, rows, LANES)
        span = pl.ds(2 * pair, 2)
        stores.append(
            pltpu.make_async_copy(sent_ref.at[:, span], out_ref.at[:, span], out_sem.at[pair])
        )
        stores[pair].start()
    for store in stores:
        store.wait()

def picked_rows(ids, factors):
    tasks, rows = ids.shape
    blocks, entries, _ = factors.shape
    shape = (tasks, 16, rows, LANES)
    factors = pltpu.with_memory_space_constraint(factors, pltpu.MemorySpace.HBM)
    return pl.pallas_call(
        pick_kernel,
        in_specs=[HELD, HBM],
        out_specs=HBM,
        out_shape=pltpu.MemorySpace.HBM(shape, BF16),
        scratch_shapes=[
            pltpu.VMEM((tasks * rows, entries), BF16),
            pltpu.VMEM((2, blocks, entries, LANES), BF16),
            pltpu.VMEM((2, entries, 2 * LANES), BF16),
            pltpu.VMEM(shape, BF16),
            pltpu.SemaphoreType.DMA((2,)),
            pltpu.SemaphoreType.DMA((8,)),
        ],
        compiler_params=ROOM,
        cost_estimate=cost(2 * tasks * rows * entries * 16 * LANES, 8 << 20),
        name="pick",
    )(ids, factors)


def sort_kernel(all_ref, row_ref, in_ref, out_ref, low_ref, part_ref, name_ref, rank_ref, slot_ref):
    step = pl.program_id(0)
    tokens = all_ref.shape[1]
    width, tile = out_ref.shape
    count = 128
    per_row = tokens // count

    @pl.when(step == 0)
    def _():
        before = one_where(iota((256, 256), 0) < iota((256, 256), 1))
        carry = jnp.zeros((count, 1), F32)
        for at in range(0, tokens, 256):
            rows = all_ref[:, at : at + 256]
            hot = jnp.where(iota((count, 256), 0) == rows, 1.0, 0.0)
            seen = product(hot.astype(BF16), before) + carry
            rank = jnp.sum(hot * seen, axis=0, keepdims=True).astype(jnp.int32)
            carry = carry + jnp.sum(hot, axis=1, keepdims=True)
            slot = rows * per_row + rank
            slot_ref[:, at : at + 256] = slot
            rank_ref[at // 256] = slot

    total = jnp.zeros((tile, width), F32)
    for at in range(0, tokens, 1024):
        place = iota((tile, 1024), 0) + step * tile
        hot = one_where(place == slot_ref[:, at : at + 1024])
        total = total + product(hot, in_ref[at : at + 1024, :])
    out_ref[...] = total.T.astype(BF16)

    for at in range(0, tile, 256):
        slot = rank_ref[step * (tile // 256) + at // 256]
        slot = jnp.broadcast_to(slot.astype(F32), (LANES, 256)).T.astype(jnp.int32)
        span = slice(at, at + 256)
        lane = iota((256, LANES), 1)
        low_ref[span, :LANES] = one_where((slot & 255) == lane)
        low_ref[span, LANES:] = one_where((slot & 255) == lane + LANES)
        part_ref[span, :] = (slot >> 8).astype(F32).astype(BF16)
        name_ref[span, :] = (slot // per_row).astype(F32).astype(BF16)


def sorted_tokens(local_row, inputs):
    tokens, width = inputs.shape
    tile = 512
    wide = lambda lanes: jax.ShapeDtypeStruct((tokens, lanes), BF16)
    return pl.pallas_call(
        sort_kernel,
        grid=(tokens // tile,),
        in_specs=[
            pl.BlockSpec((1, tokens), lambda i: (0, 0)),
            pl.BlockSpec((1, tile), lambda i: (0, i)),
            pl.BlockSpec((tokens, width), lambda i: (0, 0)),
        ],
        out_specs=[
            pl.BlockSpec((width, tile), lambda i: (0, i)),
            pl.BlockSpec((tile, 256), lambda i: (i, 0)),
            pl.BlockSpec((tile, LANES), lambda i: (i, 0)),
            pl.BlockSpec((tile, LANES), lambda i: (i, 0)),
        ],
        out_shape=[jax.ShapeDtypeStruct((width, tokens), BF16), wide(256), wide(LANES), wide(LANES)],
        scratch_shapes=[
            pltpu.VMEM((tokens // 256, 1, 256), jnp.int32),
            pltpu.VMEM((1, tokens), jnp.int32),
        ],
        cost_estimate=cost(2 * tokens * tokens * width, 16 << 20),
        name="sort",
    )(local_row, local_row, inputs)


def entry_kernel(in_ref, block_ref, out_ref):
    rows = block_ref.shape[3]
    part = 16
    slots = in_ref.shape[1] * part // rows
    match = iota((part, slots), 0) == iota((part, slots), 1) // (slots // part)
    for at in range(0, rows, part):
        span = slice(at, at + part)
        factor = jnp.concatenate(
            [block_ref[0, :, q, span].reshape(RANK * part, LANES) for q in range(4)], axis=1
        )
        first = at // part * slots
        scores = product(factor, in_ref[:, first : first + slots])
        scores = jnp.where(match[None], scores.reshape(RANK, part, slots), 0.0)
        coef = jnp.sum(scores, axis=1).astype(out_ref.dtype)
        for piece in range(0, slots, 256):
            out_ref[(first + piece) // 256] = coef[:, piece : piece + 256]


def rank_parts(inputs, blocks):
    width, tokens = inputs.shape
    rows = blocks.shape[3]
    steps = 2
    return pl.pallas_call(
        entry_kernel,
        grid=(steps,),
        in_specs=[
            pl.BlockSpec((width, tokens // steps), lambda i: (0, i)),
            pl.BlockSpec((1, RANK, 4, rows // steps, LANES), lambda i: (0, 0, 0, i, 0)),
        ],
        out_specs=pl.BlockSpec((tokens // steps // 256, RANK, 256), lambda i: (i, 0, 0)),
        out_shape=jax.ShapeDtypeStruct((tokens // 256, RANK, 256), BF16),
        name="entry",
    )(inputs, blocks)


def order_kernel(block_ref, out_ref):
    out_at = iota((256, 256), 0)
    perm = one_where(iota((256, 256), 1) == (out_at & 15) * 16 + (out_at >> 4))
    for at in range(0, block_ref.shape[3], 16):
        piece = jnp.concatenate(
            [block_ref[0, :, q, at : at + 16].reshape(RANK * 16, LANES) for q in range(4)],
            axis=1,
        )
        out_ref[at * RANK : at * RANK + 256] = product(perm, piece).astype(BF16)


def ordered_exit(blocks):
    rows = blocks.shape[3]
    part = rows // 2
    return pl.pallas_call(
        order_kernel,
        grid=(rows // part,),
        in_specs=[pl.BlockSpec((1, RANK, 4, part, LANES), lambda i: (1, 0, 0, i, 0))],
        out_specs=pl.BlockSpec((part * RANK, 4 * LANES), lambda i: (i, 0)),
        out_shape=jax.ShapeDtypeStruct((rows * RANK, 4 * LANES), BF16),
        compiler_params=ROOM,
        name="order",
    )(blocks)


def exit_kernel(coef_ref, low_ref, part_ref, name_ref, base_ref, factor_ref, out_ref):
    tile = base_ref.shape[0]
    depth = factor_ref.shape[0]
    group = lane_group(tile)
    zero = jnp.zeros((tile, LANES), F32)
    values = product(low_ref[...], coef_ref[...].reshape(256, 256), 1, 1)
    part = part_ref[...].astype(F32)
    group32 = group.astype(F32)
    mine = jnp.where(part == group32, values[:, :LANES], zero)
    mine = mine + jnp.where(part == group32 + 8.0, values[:, LANES:], zero)
    fold = one_where((iota((LANES, LANES), 0) & 15) == (iota((LANES, LANES), 1) & 15))
    coef = product(mine.astype(BF16), fold).astype(BF16)
    name = name_ref[...]
    spread = jnp.concatenate(
        [
            jnp.where(name == group + jnp.asarray(at, BF16), coef, jnp.zeros_like(coef))
            for at in range(0, depth // RANK, 8)
        ],
        axis=1,
    )
    update = product(spread, factor_ref[...])
    base = base_ref[...].astype(F32)
    out_ref[...] = (base + update * (1.0 / math.sqrt(RANK))).astype(BF16)


def apply_update(coefs, low, part, name, base, factors):
    tokens, width = base.shape
    tile = 1024
    low, part, name, base = (
        pltpu.with_memory_space_constraint(array, pltpu.MemorySpace.HBM)
        for array in (low, part, name, base)
    )
    return pl.pallas_call(
        exit_kernel,
        grid=(tokens // tile,),
        in_specs=[
            HELD,
            pl.BlockSpec((tile, 256), lambda i: (i, 0)),
            pl.BlockSpec((tile, LANES), lambda i: (i, 0)),
            pl.BlockSpec((tile, LANES), lambda i: (i, 0)),
            pl.BlockSpec((tile, width), lambda i: (i, 0)),
            HELD,
        ],
        out_specs=pl.BlockSpec((tile, width), lambda i: (i, 0)),
        out_shape=jax.ShapeDtypeStruct((tokens, width), BF16),
        compiler_params=ROOM,
        name="exit",
    )(coefs, low, part, name, base, factors)


def to_all(shard, axis):
    length = lax.axis_size(axis)
    return lax.all_to_all(
        jnp.broadcast_to(shard[None], (length, *shard.shape)), axis, 0, 0, tiled=True
    )


def on_device(
    task_ids,
    embed_table,
    trunk_weight,
    trunk_bias,
    head_weight,
    head_bias,
    token_row,
    inputs,
    frozen,
):
    tasks = lax.axis_size("task")
    width = lax.axis_size("width")
    rows_dev = task_ids.shape[0]
    me = lax.axis_index("task")
    ids = to_all(task_ids, "task").reshape(tasks, rows_dev)
    factors = table_factors(
        embed_table,
        trunk_weight,
        trunk_bias.reshape(1, -1),
        head_weight,
        head_bias.reshape(1, -1),
    )
    blocks = picked_rows(ids, factors)
    moved = lax.all_to_all(
        blocks.reshape(tasks * width, rows_dev, LANES), BOTH, 0, 0, tiled=True
    ).reshape(2, RANK, 4, rows_dev, LANES)

    local_row = (token_row - me * rows_dev).reshape(1, -1)
    in_order, low, part, name = sorted_tokens(local_row, inputs)
    parts = rank_parts(in_order, moved)
    pieces = lax.all_to_all(parts, "width", 0, 0, tiled=True).astype(F32)
    coef = (pieces.sum(axis=0) * (1.0 / math.sqrt(WIDTH))).astype(BF16)
    coefs = to_all(coef, "width")
    return apply_update(coefs, low, part, name, frozen, ordered_exit(moved))


def solution(mesh):
    return jax.shard_map(
        on_device,
        mesh=mesh,
        in_specs=(
            P("task"),
            P(),
            P(),
            P(),
            P(None, BOTH),
            P(BOTH),
            P("task"),
            P("task", "width"),
            P("task", "width"),
        ),
        out_specs=P("task", "width"),
        check_vma=False,
    )
```
